128 devices in a mesh: energy: 32 (over x, y, core), slab: 4 (over z).
Axes of the slice: x: 4, y: 4, z: 4, core: 2. Of those that a mesh axis runs over, the one named last changes fastest.
Arguments:
- hamiltonian: float32 [4, 2, 256, 256], P('slab'), may hold values from -1 to 1, as said below
- contact: float32 [2, 32, 2, 2, 256, 256], P(None, 'energy'), may hold values from -0.109375 to 0.109375
- hop: float32 [3, 256], replicated, may hold values from 0.4 to 1.2
- bond: int32 [3, 256], replicated, may hold values from 0 to 255, each once within a row
- shifts: int32 [4], replicated, may hold values from -3 to 3, as said below
- strength: float32 [4], replicated, may hold values from 0.1 to 0.4
- coupling: float32 [256, 256], replicated, may hold values from -0.375 to 0.375
Outputs:
- green: float32 [2, 32, 4, 2, 256, 256], P(None, 'energy', 'slab')
- self_energy: float32 [2, 32, 4, 2, 256, 256], P(None, 'energy', 'slab')
- density: float32 [4, 256], P('slab')
The draws below stay inside these ranges and needn't reach their ends.
Inputs may be any that keep to these rules, and one draw needn't show every extreme that they name: `hamiltonian`: each slab's block is Hermitian: the real part symmetric, the imaginary part antisymmetric with a zero diagonal. `shifts`: the table is 3, -3, k, -k in this order, for some k with 1 <= k < 3.
All inputs are finite; a program needn't handle non-finite values.
Results may differ from the reference program's by a relative error of at most 0.0001.
Values sent between devices are 32-bit elements; how exact they have to be, the bound alone decides.
No kernel may reach another device: no remote copies, remote signals or barrier semaphores. Data moves between devices by JAX's collectives and lax.ppermute only.
A program may use at most 128 MiB of HBM per device.

```python
import math
import jax
import jax.numpy as jnp
from jax import lax

B = 256
EROWS = 2
ITERS = 1
NEWTON = 2
MODES = 4
KMAX = 3
SLABS = 4
ECOLS = 32
ENERGIES = 64


def draw_hamiltonian(key, part):
    subkeys = jax.random.split(key, 3)
    block_shape = (SLABS, B, B)
    noise_real = jnp.clip(0.03 * jax.random.normal(subkeys[0], block_shape, jnp.float32), -0.15, 0.15)
    noise_imag = jnp.clip(0.03 * jax.random.normal(subkeys[1], block_shape, jnp.float32), -0.15, 0.15)
    onsite = jax.random.uniform(subkeys[2], (SLABS, B), jnp.float32, -0.4, 0.4)
    identity = jnp.eye(B, dtype=jnp.float32)
    symmetric = 0.7071 * (noise_real + jnp.swapaxes(noise_real, 1, 2))
    skew_part = 0.7071 * (noise_imag - jnp.swapaxes(noise_imag, 1, 2))
    real_part = symmetric * (1.0 - identity) + onsite[:, :, None] * identity
    return jnp.stack([real_part, skew_part], axis=1)


def draw_shifts(key, part):
    second = jax.random.randint(key, (), 1, KMAX, dtype=jnp.int32)
    largest = jnp.full((), KMAX, dtype=jnp.int32)
    return jnp.stack([largest, -largest, second, -second]).astype(jnp.int32)


def levels(rng, dims, pieces, low, high):
    def one(dim, blocks):
        steps = jax.random.uniform(jax.random.fold_in(jax.random.fold_in(rng, 6), dim), (blocks,), jnp.float32, low / len(pieces), high / len(pieces))
        return jnp.repeat(jnp.exp(steps), dims[dim] // blocks).reshape((-1,) + (1,) * (len(dims) - dim - 1))

    gain = one(*pieces[0])
    for cut in pieces[1:]:
        gain = gain * one(*cut)
    return gain


def gaussian(own_key, extent, scale, limit, pieces=(), kind=jnp.bfloat16):
    array = scale * jax.random.normal(own_key, extent, jnp.float32)
    if pieces:
        array = array * levels(own_key, extent, pieces, -0.22, 0.18)
    return jnp.clip(array, -limit, limit).astype(kind)


def setup_inputs(seed: int = 0) -> dict:
    key_of = jax.random.split(jax.random.key(seed), 8)
    return {
        "hamiltonian": draw_hamiltonian(jax.random.fold_in(key_of[7], 71), 0),
        "contact": gaussian(key_of[1], (EROWS, ECOLS, 2, 2, B, B), (11 * B) ** -0.5, 0.109375, ((1, 32),), jnp.float32),
        "hop": jnp.clip(jnp.exp(jax.random.uniform(key_of[2], (SLABS - 1, B), jnp.float32, math.log(0.4), math.log(1.2))), 0.4, 1.2),
        "bond": jax.vmap(lambda own: jax.random.permutation(own, B))(jax.random.split(key_of[3], (SLABS - 1))).reshape((SLABS - 1, B)).astype(jnp.int32),
        "shifts": draw_shifts(jax.random.fold_in(key_of[7], 71), 0),
        "strength": jnp.clip(jnp.exp(jax.random.uniform(key_of[5], (MODES,), jnp.float32, math.log(0.1), math.log(0.4))), 0.1, 0.4),
        "coupling": gaussian(key_of[6], (B, B), B ** -0.5, 0.375, (), jnp.float32),
    }


PRECISE = lax.Precision.HIGHEST
BROADENING = 0.5
ENERGY_LOW = 4.0
ENERGY_SPAN = 1.0


def complex_product(left_block, right_block):
    real_part = jnp.matmul(left_block[..., 0, :, :], right_block[..., 0, :, :], precision=PRECISE) - jnp.matmul(left_block[..., 1, :, :], right_block[..., 1, :, :], precision=PRECISE)
    imag_part = jnp.matmul(left_block[..., 0, :, :], right_block[..., 1, :, :], precision=PRECISE) + jnp.matmul(left_block[..., 1, :, :], right_block[..., 0, :, :], precision=PRECISE)
    return jnp.stack([real_part, imag_part], axis=-3)


def left_real_part(matrix, matrix_blocks):
    return jnp.einsum("ab,...bc->...ac", matrix, matrix_blocks, precision=PRECISE)


def right_real_part(matrix_blocks, matrix):
    return jnp.einsum("...ab,bc->...ac", matrix_blocks, matrix, precision=PRECISE)


def complement_term(matrix_blocks, forward_state):
    return right_real_part(left_real_part(forward_state.T, matrix_blocks), forward_state)


def expansion_term(matrix_blocks, forward_state):
    return right_real_part(left_real_part(forward_state, matrix_blocks), forward_state.T)


def invert(matrix_blocks):
    orbitals = matrix_blocks.shape[-1]
    identity = jnp.eye(orbitals, dtype=jnp.float32)
    diag_re = jnp.diagonal(matrix_blocks[..., 0, :, :], axis1=-2, axis2=-1)
    diag_im = jnp.diagonal(matrix_blocks[..., 1, :, :], axis1=-2, axis2=-1)
    modulus = diag_re * diag_re + diag_im * diag_im
    approx = jnp.stack([(diag_re / modulus)[..., None, :] * identity, (-diag_im / modulus)[..., None, :] * identity], axis=-3)
    doubled = jnp.stack([2.0 * identity, jnp.zeros_like(identity)])
    for newton_step in range(NEWTON):
        approx = complex_product(approx, doubled - complex_product(matrix_blocks, approx))
    return approx


def green_blocks(hamiltonian, contact, self_energy, couplers, energy):
    orbitals = hamiltonian.shape[-1]
    count = energy.shape[0]
    identity = jnp.eye(orbitals, dtype=jnp.float32)
    base_diag = jnp.stack([energy[:, None, None] * identity, jnp.broadcast_to(BROADENING * identity, (count, orbitals, orbitals))], axis=1)
    matrix_blocks = []
    for slab in range(SLABS):
        block = base_diag - hamiltonian[slab] - self_energy[:, slab]
        if slab == 0:
            block = block - contact[:, 0]
        if slab == SLABS - 1:
            block = block - contact[:, 1]
        matrix_blocks.append(block)
    half = SLABS // 2
    left_green = []
    left_reduced = []
    forwarded_value = jnp.zeros_like(matrix_blocks[0])
    for slab in range(half):
        reduced = matrix_blocks[slab] - forwarded_value
        inverse_matrix = invert(reduced)
        left_reduced.append(reduced)
        left_green.append(inverse_matrix)
        forwarded_value = complement_term(inverse_matrix, couplers[slab])
    right_green = {}
    right_reduced = {}
    carried_right = jnp.zeros_like(matrix_blocks[0])
    for slab in range(SLABS - 1, half - 1, -1):
        reduced = matrix_blocks[slab] - carried_right
        inverse_matrix = invert(reduced)
        right_reduced[slab] = reduced
        right_green[slab] = inverse_matrix
        carried_right = expansion_term(inverse_matrix, couplers[slab - 1])
    final_output = [None] * SLABS
    final_output[half - 1] = invert(left_reduced[-1] - carried_right)
    final_output[half] = invert(right_reduced[half] - forwarded_value)
    for slab in range(half - 2, -1, -1):
        interior_term = expansion_term(final_output[slab + 1], couplers[slab])
        factor = left_green[slab]
        final_output[slab] = factor + complex_product(complex_product(factor, interior_term), factor)
    for slab in range(half + 1, SLABS):
        interior_term = complement_term(final_output[slab - 1], couplers[slab - 1])
        factor = right_green[slab]
        final_output[slab] = factor + complex_product(complex_product(factor, interior_term), factor)
    return jnp.stack(final_output, axis=1)


def phonon_term(green, shifts, strength, coupling):
    count = green.shape[0]
    positions = jnp.arange(count, dtype=jnp.int32)
    accum = jnp.zeros_like(green)
    for mode in range(MODES):
        source = (positions + shifts[mode]).astype(jnp.int32)
        inside = jnp.logical_and(source >= 0, source < count)
        picked = jnp.take(green, jnp.clip(source, 0, count - 1).astype(jnp.int32), axis=0)
        accum = accum + jnp.where(inside[:, None, None, None, None], strength[mode] * picked, 0.0)
    return right_real_part(left_real_part(coupling, accum), coupling.T)


def reference(hamiltonian, contact, hop, bond, shifts, strength, coupling):
    orbitals = hamiltonian.shape[-1]
    energy = ENERGY_LOW + ENERGY_SPAN * jnp.arange(ENERGIES, dtype=jnp.int32).astype(jnp.float32) / ENERGIES
    energy_rows = energy.reshape(EROWS, ECOLS)
    columns = jnp.arange(orbitals, dtype=jnp.int32)
    couplers = [hop[k][:, None] * (bond[k][:, None] == columns[None, :]).astype(jnp.float32) for k in range(SLABS - 1)]
    self_energy = jnp.zeros((ENERGIES, SLABS, 2, orbitals, orbitals), jnp.float32)
    green = self_energy

    def row_solve(packed):
        return green_blocks(hamiltonian, packed[0], packed[1], couplers, packed[2])

    for born_step in range(ITERS):
        table_self = self_energy.reshape(EROWS, ECOLS, SLABS, 2, orbitals, orbitals)
        green = lax.map(row_solve, (contact, table_self, energy_rows)).reshape(ENERGIES, SLABS, 2, orbitals, orbitals)
        self_energy = phonon_term(green, shifts, strength, coupling)
    occupation = 1.0 / (1.0 + jnp.exp(3.0 * (energy - (ENERGY_LOW + 0.5 * ENERGY_SPAN))))
    density = jnp.sum(occupation[:, None, None] * (-jnp.diagonal(green[:, :, 1], axis1=-2, axis2=-1)), axis=0)
    green_table = green.reshape(EROWS, ECOLS, SLABS, 2, orbitals, orbitals)
    self_table = self_energy.reshape(EROWS, ECOLS, SLABS, 2, orbitals, orbitals)
    return green_table, self_table, density
```

```python
import jax
import jax.numpy as jnp
from jax import lax
from jax.experimental import pallas as pl
from jax.experimental.pallas import tpu as pltpu
from jax.sharding import PartitionSpec as P

BROADENING = 0.5
ENERGY_LOW = 4.0
ENERGY_SPAN = 1.0
F32 = jnp.float32
BF16 = jnp.bfloat16
SMEM = pl.BlockSpec(memory_space=pltpu.SMEM)
VMEM = pl.BlockSpec(memory_space=pltpu.VMEM)
ROWS = 2


def dot(a, b):
    return lax.dot_general(a, b, (((1,), (0,)), ((), ())), preferred_element_type=F32)


def dot_t(a, b):
    return lax.dot_general(a, b, (((1,), (1,)), ((), ())), preferred_element_type=F32)


def split(x):
    high = x.astype(BF16)
    return high, (x - high.astype(F32)).astype(BF16)


def split_complex(pair):
    return split(pair[0]), split(pair[1])


def product(left, right):
    (arh, arl), (aih, ail) = left
    (brh, brl), (bih, bil) = right
    nih, nil = -bih, -bil
    lhs = jnp.concatenate([arh, arl, aih, ail, arh, aih], axis=1)
    real = jnp.concatenate([brh, brh, nih, nih, brl, nil], axis=0)
    imag = jnp.concatenate([bih, bih, brh, brh, bil, brl], axis=0)
    return dot(lhs, real), dot(lhs, imag)


def permuted(select, block):
    high, low = split(block)
    n = block.shape[0]
    rows = dot(select, jnp.concatenate([high, low], axis=1)).astype(BF16)
    both = dot_t(jnp.concatenate([rows[:, :n], rows[:, n:]], axis=0), select)
    return both[:n] + both[n:]


def unpacked(packed):
    turned = packed.T
    return 0.5 * (packed + turned), 0.5 * (packed - turned)


def iota(shape, axis):
    return lax.broadcasted_iota(jnp.int32, shape, axis)


def eye_mask(n):
    return iota((n, n), 0) == iota((n, n), 1)


def reciprocal(re, im):
    modulus = re * re + im * im
    return re / modulus, -im / modulus


def inverse(blocks):
    n = blocks[0][0].shape[0]
    eye = eye_mask(n)
    stage = []
    for re, im in blocks:
        dre, dim = jnp.where(eye, re, 0.0), jnp.where(eye, im, 0.0)
        row = reciprocal(jnp.sum(dre, axis=0, keepdims=True), jnp.sum(dim, axis=0, keepdims=True))
        col = reciprocal(jnp.sum(dre, axis=1, keepdims=True), jnp.sum(dim, axis=1, keepdims=True))
        ore, oim = re - dre, im - dim
        g = (ore * row[0] - oim * row[1], ore * row[1] + oim * row[0])
        stage.append((g, col, split_complex(g)))
    squares = [product(s, s) for _, _, s in stage]
    cubes = [product(s, split_complex(q)) for (_, _, s), q in zip(stage, squares)]
    out = []
    for (g, col, _), q, r in zip(stage, squares, cubes):
        tre = (q[0] - r[0]) - g[0] + jnp.where(eye, 1.0, 0.0)
        tim = (q[1] - r[1]) - g[1]
        out.append((col[0] * tre - col[1] * tim, col[0] * tim + col[1] * tre))
    return out


def setup_kernel(flags, bond_row, bond_col, hop_row, hop_col, contact, q_near, q_fi, q_fo, h_row, h_col, near, far):
    left, outer = flags[0] == 1, flags[1] == 1
    n = bond_row.shape[1]
    lanes, subs = iota((n, n), 1), iota((n, n), 0)
    forward = [bond_col[:, k : k + 1] == lanes for k in range(3)]
    turned = [bond_row[k : k + 1, :] == subs for k in range(3)]
    one = lambda mask: jnp.where(mask, 1.0, 0.0)
    steps = [jnp.where(left, one(forward[k]), one(turned[2 - k])) for k in range(3)]
    back = jnp.where(left, one(turned[0]), one(forward[2]))
    eye = one(lanes == subs)
    first = jnp.where(outer, steps[0], eye)
    partner = jnp.where(outer, steps[0], back).astype(BF16)
    near_outer = jnp.where(outer, eye, back).astype(BF16)
    steps = [s.astype(BF16) for s in steps]
    inner = dot(first.astype(BF16), steps[1]).astype(BF16)
    last = dot(inner, steps[2]).astype(BF16)
    q_near[...] = partner
    q_fi[...] = inner
    q_fo[...] = last
    near_inner = first.astype(BF16)
    carriers = [
        jnp.where(left, near_outer.astype(F32), last.astype(F32)),
        jnp.where(left, near_inner.astype(F32), inner.astype(F32)),
        jnp.where(left, inner.astype(F32), near_inner.astype(F32)),
    ]
    for k in range(3):
        moved = carriers[k] * hop_row[k : k + 1, :]
        as_col = jnp.sum(moved, axis=1, keepdims=True)
        slot = jnp.where(left, k, 2 - k)
        h_col[slot] = jnp.broadcast_to(as_col, (n, 128))
        h_row[slot] = jnp.sum(jnp.where(lanes == subs, as_col, 0.0), axis=0, keepdims=True)
    near_side = jnp.where(left, 0, 1)
    for r in range(ROWS):
        for part in range(2):
            near[r, part] = permuted(near_outer, contact[r, near_side, part])
            far[r, part] = permuted(last, contact[r, 1 - near_side, part])


def shifted_block(energy, ham, extra, eye):
    return (
        jnp.where(eye, energy, 0.0) - ham[0] - extra[0],
        jnp.where(eye, BROADENING, 0.0) - ham[1] - extra[1],
    )


def dressed(pair, h_col, h_row, slot):
    scale = h_col[slot][:, :1] * h_row[slot]
    return pair[0] * scale, pair[1] * scale


def near_kernel(flags, points, own, received, q_near, h_row, h_col, near, g_outer, inner_block):
    outer = flags[1] == 1
    eye = eye_mask(own.shape[-1])
    mine = (own[0], own[1])
    other = unpacked(permuted(q_near[...], received[...]))
    outside = [jnp.where(outer, a, b) for a, b in zip(mine, other)]
    inside = [jnp.where(outer, b, a) for a, b in zip(mine, other)]
    blocks = [shifted_block(points[r], outside, (near[r, 0], near[r, 1]), eye) for r in range(ROWS)]
    for r, g in enumerate(inverse(blocks)):
        g_outer[r, 0], g_outer[r, 1] = g
        reduced = shifted_block(points[r], inside, dressed(g, h_col, h_row, 0), eye)
        inner_block[r, 0], inner_block[r, 1] = reduced


def far_kernel(flags, points, recv_b, recv_c, q_fi, q_fo, h_row, h_col, far, g_outer, inner_block, green, density):
    outer = flags[1] == 1
    n = recv_b.shape[-1]
    eye = eye_mask(n)
    packed_o = jnp.where(outer, recv_b[...], recv_c[...])
    packed_i = jnp.where(outer, recv_c[...], recv_b[...])
    ham_o = unpacked(permuted(q_fo[...], packed_o))
    ham_i = unpacked(permuted(q_fi[...], packed_i))
    ends = inverse([shifted_block(points[r], ham_o, (far[r, 0], far[r, 1]), eye) for r in range(ROWS)])
    reduced = [shifted_block(points[r], ham_i, dressed(ends[r], h_col, h_row, 2), eye) for r in range(ROWS)]
    inner = inverse(reduced)
    middle = []
    for r in range(ROWS):
        cross = dressed(inner[r], h_col, h_row, 1)
        middle.append((inner_block[r, 0] - cross[0], inner_block[r, 1] - cross[1]))
    for r, g in enumerate(inverse(middle)):
        green[r, 0], green[r, 1] = g

    @pl.when(outer)
    def _():
        for r in range(ROWS):
            factor = (g_outer[r, 0], g_outer[r, 1])
            halves = split_complex(factor)
            term = dressed((green[r, 0], green[r, 1]), h_col, h_row, 0)
            step = product(halves, split_complex(term))
            full = product(split_complex(step), halves)
            green[r, 0] = factor[0] + full[0]
            green[r, 1] = factor[1] + full[1]

    total = jnp.zeros((1, n), F32)
    for r in range(ROWS):
        total = total - points[ROWS + r] * jnp.sum(jnp.where(eye, green[r, 1], 0.0), axis=0, keepdims=True)
    density[...] = total


def fold_kernel(coupling, summed, out):
    n = coupling.shape[-1]
    ch, cl = split(coupling[...])
    lhs = jnp.concatenate([ch, cl, ch], axis=1)
    for r in range(ROWS):
        for part in range(2):
            sh, sl = split(summed[r, part])
            th, tl = split(dot(lhs, jnp.concatenate([sh, sh, sl], axis=0)))
            out[r, part] = dot_t(jnp.concatenate([th, tl, th], axis=1), jnp.concatenate([ch, ch, cl], axis=1))


def call(kernel, shapes, operands, specs, flops):
    return pl.pallas_call(
        kernel,
        out_shape=shapes,
        in_specs=specs,
        out_specs=jax.tree.map(lambda _: VMEM, shapes),
        cost_estimate=pl.CostEstimate(flops=flops, bytes_accessed=4 << 20, transcendentals=0),
        compiler_params=pltpu.CompilerParams(vmem_limit_bytes=48 << 20),
    )(*operands)


def shaped(*shape, dtype=F32):
    return jax.ShapeDtypeStruct(shape, dtype)


def per_device(hamiltonian, contact, hop, bond, shifts, strength, coupling):
    n = hamiltonian.shape[-1]
    slabs = lax.axis_size("slab")
    slab = lax.axis_index("slab")
    columns = lax.axis_size("energy")
    column = lax.axis_index("energy")
    own = hamiltonian[0]
    packed = own[0] + own[1]
    across = [(i, slabs - 1 - i) for i in range(slabs)]
    recv_a = lax.ppermute(packed, "slab", [(i, i ^ 1) for i in range(slabs)])
    recv_b = lax.ppermute(packed, "slab", across)
    recv_c = lax.ppermute(recv_a, "slab", across)

    left = slab < slabs // 2
    outer = (slab == 0) | (slab == slabs - 1)
    flags = jnp.stack([left, outer]).astype(jnp.int32)
    position = jnp.arange(ROWS, dtype=jnp.int32) * columns + column
    energy = ENERGY_LOW + ENERGY_SPAN * position.astype(F32) / (ROWS * columns)
    occupation = 1.0 / (1.0 + jnp.exp(3.0 * (energy - (ENERGY_LOW + 0.5 * ENERGY_SPAN))))
    points = jnp.concatenate([energy, occupation])

    select = shaped(n, n, dtype=BF16)
    pair = shaped(ROWS, 2, n, n)
    q_near, q_fi, q_fo, h_row, h_col, near, far = call(
        setup_kernel,
        (select, select, select, shaped(3, 1, n), shaped(3, n, 128), pair, pair),
        (flags, bond, bond.T, hop, hop.T, contact[:, 0]),
        [SMEM] + [VMEM] * 5,
        2 * 80 * n**3,
    )
    g_outer, inner_block = call(
        near_kernel,
        (pair, pair),
        (flags, points, own, recv_a, q_near, h_row, h_col, near),
        [SMEM] * 2 + [VMEM] * 6,
        2 * 60 * n**3,
    )
    green, partial = call(
        far_kernel,
        (pair, shaped(1, n)),
        (flags, points, recv_b, recv_c, q_fi, q_fo, h_row, h_col, far, g_outer, inner_block),
        [SMEM] * 2 + [VMEM] * 9,
        2 * 240 * n**3,
    )

    core = column % 2
    even = core == 0
    lowest, highest = column <= 1, column >= columns - 2

    def ring(route):
        return [(i, route(i) % columns) for i in range(columns)]

    def aligned(block, from_above):
        zero = jnp.zeros_like(block[:1])
        up = jnp.concatenate([block[1:], zero], axis=0)
        down = jnp.concatenate([zero, block[:-1]], axis=0)
        return jnp.where(from_above & highest, up, jnp.where(~from_above & lowest, down, block))

    def pick(when_even, when_odd):
        return jnp.where(even, when_even, when_odd)

    wide = shifts[2] == 2
    far_scale, step_scale = pick(strength[0], strength[1]), pick(strength[2], strength[3])
    mate = lax.ppermute(green, "energy", ring(lambda i: i ^ 1))
    beyond = lax.ppermute(green, "energy", ring(lambda i: i - 1 if i % 2 == 0 else i + 1))
    beyond = aligned(beyond, ~even)
    same = jnp.where(wide, step_scale, 0.0) * green + far_scale * mate
    same = lax.ppermute(same, "energy", ring(lambda i: i - 2 if i % 2 == 0 else i + 2))
    same = aligned(same, even)
    cross_far, cross_step = pick(strength[1], strength[0]), pick(strength[3], strength[2])
    relay = (
        cross_far * beyond
        + jnp.where(wide, cross_step, 0.0) * green
        + jnp.where(wide, 0.0, cross_step) * mate
    )
    relay = lax.ppermute(relay, "energy", ring(lambda i: i + 2 if i % 2 == 0 else i - 2))
    relay = aligned(relay, ~even)
    summed = same + relay + jnp.where(wide, 0.0, step_scale) * mate
    self_energy = call(fold_kernel, pair, (coupling, summed), [VMEM] * 2, 2 * 24 * n**3)

    density = partial
    for distance in (1, 2, 4, 8, 16):
        density = density + lax.ppermute(density, "energy", [(i, i ^ distance) for i in range(columns)])
    return (green[:, None, None], self_energy[:, None, None], density)


def solution(mesh):
    in_specs = (
        P("slab", None, None, None),
        P(None, "energy", None, None, None, None),
        P(),
        P(),
        P(),
        P(),
        P(),
    )
    out_specs = (
        P(None, "energy", "slab", None, None, None),
        P(None, "energy", "slab", None, None, None),
        P("slab", None),
    )
    return jax.shard_map(
        per_device, mesh=mesh, in_specs=in_specs, out_specs=out_specs, check_vma=False
    )
```
